32 devices in a mesh: grp: 2 (over y), cell: 4 (over z), snap: 2 (over x), var: 2 (over core).
Axes of the slice: x: 2, y: 2, z: 4, core: 2. Of those that a mesh axis runs over, the one named last changes fastest.
Arguments:
- q_true: bfloat16 [64, 10, 2048], P(('snap', 'var'), 'grp', 'cell'), parts along dimension 1, may hold values from -6 to 6
- coeffs: bfloat16 [64, 256], P(('snap', 'var'), 'grp'), parts along dimension 1, may hold values from -0.5 to 0.5
- basis: bfloat16 [128, 10, 2048], P(('snap', 'var'), 'grp', 'cell'), parts along dimension 1, may hold values from -6 to 6
- weights: float32 [10, 2048], P('grp', 'cell'), parts along dimension 0, may hold values from 0.0029646354 to 0.029646354
- geometry: float32 [12, 2048], P('grp', 'cell'), parts along dimension 0, may hold values from 0.2 to 1
- neighbors: int32 [12, 2048], P('grp', 'cell'), parts along dimension 0, may hold values from 0 to 767, as said below
- send_rows: int32 [4, 4, 128], P('cell', 'grp'), parts along dimension 1, may hold values from 0 to 511, as said below
- block_count: int32 [4, 2], P('cell', 'grp'), parts along dimension 1, may hold values from 2 to 4
Outputs:
- closure: float32 [64, 256], P(('snap', 'var'), 'grp'), parts along dimension 1
The draws below stay inside these ranges and needn't reach their ends.
There are 2 independent parts, one for each index of `grp`. The reference program is written for one: setup_inputs(seed, part) draws one part's arguments, and reference() takes and returns one part's arrays. A program takes and returns all parts, laid end to end along the dimension named above; each array names one. Nothing has to cross between parts.
Inputs may be any that keep to these rules, and one draw needn't show every extreme that they name: neighbors[k, c] indexes a list made of the 512 cells of c's own cell shard, then the 128 cells received from the shard before, then the 128 cells received from the shard after. `send_rows`: indices local to the sending cell shard.
All inputs are finite; a program needn't handle non-finite values.
Results may differ from the reference program's by a relative error of at most 0.00091.
Values may be sent and summed in bfloat16 or wider, within the bound.
A program may use at most 64 MiB of HBM per device.

```python
import math
import jax
import jax.numpy as jnp
from jax import lax

R = 128
NV = 5
K = 6
BLOCK = 128
BLK_DEV = 4
CELLS_DEV = 512
HALO = 128
CELLS = 2048
SNAPS = 64
N_CELL = 4


def draw_neighbors(key, part):
    keys = jax.random.split(key, 3)
    positions = jnp.arange(CELLS, dtype=jnp.int32) % CELLS_DEV
    offset = jax.random.randint(keys[0], (K, CELLS), -BLOCK, BLOCK + 1)
    nearby = jnp.clip(positions[None, :] + offset, 0, CELLS_DEV - 1)
    remote = jax.random.randint(keys[1], (K, CELLS), CELLS_DEV, CELLS_DEV + 2 * HALO)
    choose = jax.random.randint(keys[2], (K, CELLS), 0, 8) == 0
    result = jnp.where(choose, remote, nearby)
    faces = jnp.arange(K, dtype=jnp.int32)[:, None]
    result = jnp.where((faces == K - 1) & (positions[None, :] == 0), CELLS_DEV + 2 * HALO - 1, result)
    result = jnp.where((faces == K - 1) & (positions[None, :] == 1), 0, result)
    return result.astype(jnp.int32)


def draw_send_rows(key, part):
    keys = jax.random.split(key, 2)
    lower = jax.random.randint(keys[0], (N_CELL, 1, HALO), 0, 2 * HALO)
    upper = jax.random.randint(keys[1], (N_CELL, 1, HALO), CELLS_DEV - 2 * HALO, CELLS_DEV)
    slots = jnp.arange(HALO, dtype=jnp.int32)[None, None, :]
    lower = jnp.where(slots == 0, 0, lower)
    upper = jnp.where(slots == 0, CELLS_DEV - 1, upper)
    return jnp.concatenate([lower, upper], axis=1).astype(jnp.int32)


def draw_block_count(key, part):
    keys = jax.random.split(key, 2)
    counts = jax.random.randint(keys[0], (N_CELL, 1), BLK_DEV // 2, BLK_DEV + 1)
    chosen = jax.random.randint(keys[1], (), 0, N_CELL)
    rows = jnp.arange(N_CELL, dtype=jnp.int32)[:, None]
    return jnp.where(rows == chosen, BLK_DEV, counts).astype(jnp.int32)


def block_scale(own_key, dims, cuts, least, high):
    def one(position, shards_of):
        steps = jax.random.uniform(jax.random.fold_in(jax.random.fold_in(own_key, 6), position), (shards_of,), jnp.float32, least / len(cuts), high / len(cuts))
        return jnp.repeat(jnp.exp(steps), dims[position] // shards_of).reshape((-1,) + (1,) * (len(dims) - position - 1))

    level = one(*cuts[0])
    for cut in cuts[1:]:
        level = level * one(*cut)
    return level


def bell_draw(own_key, extent, spread, reach, cuts=(), kind=jnp.bfloat16):
    factor_of = block_scale(own_key, extent, cuts, -0.22, 0.18) if cuts else 1.0
    values = jax.random.normal(own_key, extent, jnp.float32) * spread * factor_of
    return jnp.minimum(jnp.maximum(values, -reach), reach).astype(kind)


def setup_inputs(seed: int = 0, part: int = 0) -> dict:
    seeds = jax.random.split(jax.random.key(seed), 9)
    own_keys = jax.random.split(jax.random.fold_in(seeds[8], part), 9)
    return {
        "q_true": bell_draw(own_keys[0], (SNAPS, NV, CELLS), 1.0, 6.0, ((0, 4), (2, 4))),
        "coeffs": bell_draw(own_keys[1], (SNAPS, R), R ** -0.5, 0.5, ((0, 4),)),
        "basis": bell_draw(own_keys[2], (R, NV, CELLS), 1.0, 6.0, ((0, 4), (2, 4))),
        "weights": jnp.clip(jnp.exp(math.log(0.029646354) - 2.3025851 * jax.random.uniform(own_keys[3], (NV, CELLS), jnp.float32) ** block_scale(own_keys[3], (NV, CELLS), ((1, 4),), -0.2, 0.2)), 0.0029646354, 0.029646354),
        "geometry": jnp.clip(0.2 + 0.8 * jax.random.uniform(own_keys[4], (K, CELLS), jnp.float32) ** block_scale(own_keys[4], (K, CELLS), ((1, 4),), -0.2, 0.2), 0.2, 1.0),
        "neighbors": draw_neighbors(jax.random.fold_in(jax.random.fold_in(seeds[8], part), 71), part),
        "send_rows": draw_send_rows(jax.random.fold_in(jax.random.fold_in(seeds[8], part), 71), part),
        "block_count": draw_block_count(jax.random.fold_in(jax.random.fold_in(seeds[8], part), 71), part),
    }


def face_flux(extended, geometry, neighbors):
    cell_count = geometry.shape[1]
    var_count = extended.shape[1]
    own_cells = extended[:, :, :cell_count]
    product = extended * extended[:, 1:2, :]
    own_product = product[:, :, :cell_count]
    stacked = jnp.concatenate([extended, product], axis=1)
    running = jnp.zeros(own_cells.shape, jnp.float32)
    for face_index in range(K):
        taken = jnp.take(stacked, neighbors[face_index], axis=2)
        beside = taken[:, :var_count]
        beside_product = taken[:, var_count:]
        running = running + geometry[face_index] * (0.5 * (own_product + beside_product) - 0.5 * (beside - own_cells))
    return running


def reference(q_true, coeffs, basis, weights, geometry, neighbors, send_rows, block_count):
    snap_count = q_true.shape[0]
    basis_flat = basis.reshape(R, NV * CELLS)
    rebuilt = jnp.dot(coeffs, basis_flat, preferred_element_type=jnp.float32).astype(jnp.bfloat16)
    rebuilt = rebuilt.reshape(snap_count, NV, CELLS)

    def blocked(field):
        return field.reshape(field.shape[0], NV, N_CELL, CELLS_DEV).transpose(2, 0, 1, 3)

    true_blocks = blocked(q_true)
    rebuilt_blocks = blocked(rebuilt)
    basis_blocks = blocked(basis)
    weight_blocks = weights.reshape(NV, N_CELL, CELLS_DEV).transpose(1, 0, 2)
    geometry_blocks = geometry.reshape(K, N_CELL, CELLS_DEV).transpose(1, 0, 2)
    neighbor_blocks = neighbors.reshape(K, N_CELL, CELLS_DEV).transpose(1, 0, 2)

    def rim_rows(blocks, which):
        return jax.vmap(lambda block, rows: jnp.take(block, rows, axis=2))(blocks, send_rows[:, which, :])

    def extend(blocks):
        to_prev = rim_rows(blocks, 0)
        to_next = rim_rows(blocks, 1)
        zero_rim = jnp.zeros_like(to_next[:1])
        from_prev = jnp.concatenate([zero_rim, to_next[:-1]], axis=0)
        from_next = jnp.concatenate([to_prev[1:], zero_rim], axis=0)
        return jnp.concatenate([blocks, from_prev, from_next], axis=3)

    true_ext = extend(true_blocks)
    rebuilt_ext = extend(rebuilt_blocks)
    positions = jnp.arange(CELLS_DEV, dtype=jnp.int32)

    def one_shard(inputs):
        true_part, rebuilt_part, basis_part, weight_part, geometry_part, neighbor_part, count_row = inputs
        flux_true = face_flux(true_part.astype(jnp.float32), geometry_part, neighbor_part)
        flux_rebuilt = face_flux(rebuilt_part.astype(jnp.float32), geometry_part, neighbor_part)
        live = (positions < count_row[0] * BLOCK).astype(jnp.float32)
        weighted = (weight_part * live * (flux_true - flux_rebuilt)).astype(jnp.bfloat16)
        return jnp.einsum("svc,rvc->sr", weighted.astype(jnp.float32), basis_part.astype(jnp.float32))

    partials = lax.map(one_shard, (true_ext, rebuilt_ext, basis_blocks, weight_blocks, geometry_blocks, neighbor_blocks, block_count))
    return jnp.sum(partials, axis=0)
```

```python
import functools

import jax
import jax.numpy as jnp
from jax import lax
from jax.experimental import pallas as pl
from jax.experimental.pallas import tpu as pltpu
from jax.sharding import PartitionSpec as P

BLOCK = 128
ROWS = 32
MESH = pl.DeviceIdType.MESH
F32 = jnp.float32
BF16 = jnp.bfloat16


def dot(a, b):
    return jnp.dot(a, b, preferred_element_type=F32)


def kernel(
    fused, n_cell, q_hbm, co_hbm, basis_hbm, w_hbm, geo_hbm, nb_hbm, rows_hbm, bc_hbm, out,
    q, co, w, geo, nb, rows, bc, whole, onehot, mat_hi, mat_lo, rim, halo, field_s, diff_hi, diff_lo, parts,
    in_sem, own_sem, send_x, recv_x, send_c, recv_c, send_f, recv_f, send_h, recv_h, send_p, recv_p,
):
    var_count, snaps, cells = q.shape
    faces = geo.shape[0]
    modes = whole.shape[1]
    own_modes = basis_hbm.shape[1]
    sent = rows.shape[-1]
    ext = cells + 2 * sent
    z = lax.axis_index("cell")
    x = lax.axis_index("snap")
    c = lax.axis_index("var")
    order = [1] + [v for v in range(var_count) if v != 1]

    peers = [{"cell": lax.rem(z + d, n_cell)} for d in range(1, n_cell)]
    if fused:
        peers += [{"snap": 1 - x}, {"var": 1 - c}]
    barrier = pltpu.get_barrier_semaphore()
    for peer in peers:
        pl.semaphore_signal(barrier, inc=1, device_id=peer, device_id_type=MESH)

    loads = []
    for i, (src, dst) in enumerate(
        ((rows_hbm, rows), (q_hbm, q), (nb_hbm, nb), (geo_hbm, geo), (co_hbm, co), (w_hbm, w), (bc_hbm, bc))
    ):
        loads.append(pltpu.make_async_copy(src, dst, in_sem.at[i]))
        loads[-1].start()
    l_rows, l_q, l_nb, l_geo, l_co, l_w, l_bc = loads
    pl.semaphore_wait(barrier, len(peers))

    def mode_rows(snap, var):
        return pl.ds(pl.multiple_of((snap * 2 + var) * own_modes, own_modes), own_modes)

    own, across, to_core, forward = {}, {}, {}, {}
    if fused:
        mine = mode_rows(x, c)
        theirs = mode_rows(1 - x, c)

        def remote(src, dst, sends, recvs, v, peer):
            return pltpu.make_async_remote_copy(
                src_ref=src, dst_ref=dst, send_sem=sends.at[v], recv_sem=recvs.at[v],
                device_id=peer, device_id_type=MESH,
            )

        for v in order:
            across[v] = remote(basis_hbm.at[v], whole.at[v, mine], send_x, recv_x, v, {"snap": 1 - x})
            across[v].start()
        for v in order:
            to_core[v] = remote(basis_hbm.at[v], whole.at[v, mine], send_c, recv_c, v, {"var": 1 - c})
            to_core[v].start()
            own[v] = pltpu.make_async_copy(basis_hbm.at[v], whole.at[v, mine], own_sem.at[v])
            own[v].start()
            forward[v] = remote(whole.at[v, theirs], whole.at[v, theirs], send_f, recv_f, v, {"var": 1 - c})
    else:
        for v in order:
            own[v] = pltpu.make_async_copy(basis_hbm.at[v], whole.at[v], own_sem.at[v])
            own[v].start()

    def rim_copy(slot, side, src, dst):
        return pltpu.make_async_remote_copy(
            src_ref=src, dst_ref=dst, send_sem=send_h.at[slot, side], recv_sem=recv_h.at[slot, 1 - side],
            device_id={"cell": lax.rem(z + n_cell + 2 * side - 1, n_cell)}, device_id_type=MESH,
        )

    def rim_pair(field, v):
        if v is None:
            return [rim_copy(0, s, rim.at[0, s], halo.at[0, 1 - s]) for s in (0, 1)]
        return [rim_copy(1 + v, s, rim.at[1, s, v], halo.at[1, 1 - s, v]) for s in (0, 1)]

    def start_pair(pair):
        pl.when(z > 0)(lambda: pair[0].start())
        pl.when(z < n_cell - 1)(lambda: pair[1].start())

    @pl.when(z == 0)
    def _():
        halo[:, 0] = jnp.zeros(halo[:, 0].shape, BF16)

    @pl.when(z == n_cell - 1)
    def _():
        halo[:, 1] = jnp.zeros(halo[:, 1].shape, BF16)

    l_rows.wait()
    place = lax.broadcasted_iota(jnp.int32, (cells, sent), 0)
    for side in (0, 1):
        onehot[:, side * sent:(side + 1) * sent] = jnp.where(
            place == rows[0, side:side + 1, :], 1.0, 0.0
        ).astype(BF16)
    l_q.wait()
    true_rim = dot(q[...].reshape(var_count * snaps, cells), onehot[...]).astype(BF16)
    true_rim = true_rim.reshape(var_count, snaps, 2 * sent)
    for side in (0, 1):
        rim[0, side] = true_rim[:, :, side * sent:(side + 1) * sent]
    true_pair = rim_pair(0, None)
    start_pair(true_pair)

    l_nb.wait()
    l_geo.wait()

    def face_rows(i, carry):
        first = pl.multiple_of(i * ROWS, ROWS)
        place = lax.broadcasted_iota(jnp.int32, (ROWS, cells), 0) + first
        total = jnp.zeros((ROWS, cells), F32)
        for k in range(faces):
            total += jnp.where(nb[k:k + 1, :] == place, 0.5 * geo[k:k + 1, :], 0.0)
        high = total.astype(BF16)
        mat_hi[pl.ds(first, ROWS), :] = high
        mat_lo[pl.ds(first, ROWS), :] = (total - high.astype(F32)).astype(BF16)
        return carry

    steps = ext // ROWS
    done = 0
    for i, v in enumerate(order):
        upto = steps * (i + 1) // var_count
        lax.fori_loop(done, upto, face_rows, 0)
        done = upto
        if fused:
            across[v].wait_recv()
            forward[v].start()

    l_co.wait()
    pairs = []
    true_one = true_up = rebuilt_up = None
    for v in order:
        own[v].wait()
        if fused:
            to_core[v].wait_recv()
            forward[v].wait_recv()
        rebuilt = dot(co[...], whole[v]).astype(BF16)
        picked = dot(rebuilt, onehot[...]).astype(BF16)
        for side in (0, 1):
            rim[1, side, v] = picked[:, side * sent:(side + 1) * sent]
        pair = rim_pair(1, v)
        start_pair(pair)
        pairs.append(pair)
        e_true = q[v].astype(F32)
        e_rebuilt = rebuilt.astype(F32)
        if v == 1:
            true_up, rebuilt_up = e_true, e_rebuilt
        field_s[v] = e_true * (true_up + 1.0) - e_rebuilt * (rebuilt_up + 1.0)
        diff = e_true * (true_up - 1.0) - e_rebuilt * (rebuilt_up - 1.0)
        high = diff.astype(BF16)
        diff_hi[v, :, :cells] = high
        diff_lo[v, :, :cells] = (diff - high.astype(F32)).astype(BF16)

    lines = var_count * snaps

    def gathered(lo, hi):
        top = diff_hi[:, :, lo:hi].reshape(lines, hi - lo)
        low = diff_lo[:, :, lo:hi].reshape(lines, hi - lo)
        both = dot(jnp.concatenate([top, low], axis=0), mat_hi[lo:hi, :])
        return both[:lines] + both[lines:] + dot(top, mat_lo[lo:hi, :])

    near = gathered(0, cells)
    l_w.wait()
    l_bc.wait()
    coefficient = 0.5 * jnp.sum(geo[...], axis=0, keepdims=True)
    spot = lax.broadcasted_iota(jnp.int32, (1, cells), 1)
    live = jnp.where(spot < bc[...] * BLOCK, 1.0, 0.0)
    scale = w[...] * live

    for pair in [true_pair] + pairs:
        pl.when(z < n_cell - 1)(lambda: pair[0].wait_recv())
        pl.when(z > 0)(lambda: pair[1].wait_recv())
    for side in (0, 1):
        true_up = halo[0, side, 1].astype(F32) - 1.0
        rebuilt_up = halo[1, side, 1].astype(F32) - 1.0
        for v in range(var_count):
            diff = halo[0, side, v].astype(F32) * true_up - halo[1, side, v].astype(F32) * rebuilt_up
            high = diff.astype(BF16)
            first = cells + side * sent
            diff_hi[v, :, first:first + sent] = high
            diff_lo[v, :, first:first + sent] = (diff - high.astype(F32)).astype(BF16)
    flux = (near + gathered(cells, ext)).reshape(var_count, snaps, cells)
    total = jnp.zeros((snaps, modes), F32)
    for v in range(var_count):
        weighted = (scale[v:v + 1, :] * (coefficient * field_s[v] + flux[v])).astype(BF16)
        total += lax.dot_general(
            weighted, whole[v], (((1,), (1,)), ((), ())), preferred_element_type=F32
        )

    parts[0] = total
    sums = []
    for d in range(1, n_cell):
        copy = pltpu.make_async_remote_copy(
            src_ref=parts.at[0], dst_ref=parts.at[d], send_sem=send_p.at[d - 1], recv_sem=recv_p.at[d - 1],
            device_id={"cell": lax.rem(z + d, n_cell)}, device_id_type=MESH,
        )
        copy.start()
        sums.append(copy)
    if fused:
        for v in order:
            across[v].wait_send()
            to_core[v].wait_send()
            forward[v].wait_send()
    for pair in [true_pair] + pairs:
        pl.when(z > 0)(lambda: pair[0].wait_send())
        pl.when(z < n_cell - 1)(lambda: pair[1].wait_send())
    for copy in sums:
        copy.wait_recv()
        copy.wait_send()
    out[...] = jnp.sum(parts[...], axis=0)


def local(mesh, q_true, coeffs, basis, weights, geometry, neighbors, send_rows, block_count):
    snaps, var_count, cells = q_true.shape
    own_modes = basis.shape[0]
    faces = geometry.shape[0]
    modes = coeffs.shape[1]
    sent = send_rows.shape[-1]
    ext = cells + 2 * sent
    n_cell = mesh.shape["cell"]
    fused = mesh.shape["snap"] == 2 and mesh.shape["var"] == 2 and own_modes % 16 == 0
    if not fused:
        basis = lax.all_gather(basis, ("snap", "var"), axis=0, tiled=True)
    dma = pltpu.SemaphoreType.DMA
    vmem = pltpu.VMEM
    scratch = [
        vmem((var_count, snaps, cells), BF16),
        vmem((snaps, modes), BF16),
        vmem((var_count, cells), F32),
        vmem((faces, cells), F32),
        vmem((faces, cells), jnp.int32),
        vmem((1, 2, sent), jnp.int32),
        vmem((1, 1), jnp.int32),
        vmem((var_count, modes, cells), BF16),
        vmem((cells, 2 * sent), BF16),
        vmem((ext, cells), BF16),
        vmem((ext, cells), BF16),
        vmem((2, 2, var_count, snaps, sent), BF16),
        vmem((2, 2, var_count, snaps, sent), BF16),
        vmem((var_count, snaps, cells), F32),
        vmem((var_count, snaps, ext), BF16),
        vmem((var_count, snaps, ext), BF16),
        vmem((n_cell, snaps, modes), F32),
        dma((7,)),
        dma((var_count,)),
    ]
    scratch += [dma((var_count,)) for _ in range(6)]
    scratch += [dma((1 + var_count, 2)), dma((1 + var_count, 2)), dma((n_cell - 1,)), dma((n_cell - 1,))]
    return pl.pallas_call(
        functools.partial(kernel, fused, n_cell),
        out_shape=jax.ShapeDtypeStruct((snaps, modes), F32),
        in_specs=[pl.BlockSpec(memory_space=pl.ANY)] * 8,
        out_specs=pl.BlockSpec(memory_space=pltpu.VMEM),
        scratch_shapes=scratch,
        compiler_params=pltpu.CompilerParams(
            collective_id=0, has_side_effects=True, vmem_limit_bytes=32 * 1024 * 1024
        ),
        name="closure",
    )(
        jnp.transpose(q_true, (1, 0, 2)), coeffs, jnp.transpose(basis, (1, 0, 2)),
        weights, geometry, neighbors, send_rows, block_count,
    )


def solution(mesh):
    in_specs = (
        P(("snap", "var"), "grp", "cell"),
        P(("snap", "var"), "grp"),
        P(("snap", "var"), "grp", "cell"),
        P("grp", "cell"),
        P("grp", "cell"),
        P("grp", "cell"),
        P("cell", "grp", None),
        P("cell", "grp"),
    )
    out_specs = P(("snap", "var"), "grp")
    return jax.shard_map(
        functools.partial(local, mesh), mesh=mesh, in_specs=in_specs, out_specs=out_specs, check_vma=False
    )
```
